32 devices in a mesh: prow: 4 (over y, x), pcol: 8 (over z, core).
Axes of the slice: x: 2, y: 2, z: 4, core: 2. Of those that a mesh axis runs over, the one named last changes fastest.
Arguments:
- ancestor: float32 [12288, 12288], P('prow', 'pcol'), may hold values from -448 to 15360, as said below
- factor: bfloat16 [2, 12288, 256], P(None, 'prow'), may hold values from -0.0009765625 to 0.0009765625
- inverse_diag: bfloat16 [2, 256, 256], replicated, may hold values from -6 to 6
- block_mask: int32 [2, 48], replicated, may hold values 0 or 1
Outputs:
- column_block: float32 [2, 12288, 256], P(None, ('prow', 'pcol'))
- diagonal: float32 [2, 256, 256], replicated
The draws below stay inside these ranges and needn't reach their ends.
Inputs may be any that keep to these rules, and one draw needn't show every extreme that they name: `ancestor`: symmetric.
All inputs are finite; a program needn't handle non-finite values.
Results may differ from the reference program's by a relative error of at most 0.0003.
Values may be sent and summed in bfloat16 or wider, within the bound.
A program may use at most 64 MiB of HBM per device.

```python
import math
import jax
import jax.numpy as jnp
from jax import lax

WIDTH = 256
NB = 48
SN = 2
ORDER = 12288


def draw_ancestor(key, part):
    order = NB * WIDTH
    first_key = jax.random.fold_in(jax.random.fold_in(key, 17), 0)
    noise = jnp.clip(jax.random.normal(first_key, (order, order), jnp.float32), -4.0, 4.0)
    base = (noise + noise.T) * (0.5 * order / (3.0 * math.sqrt(2.0 * order)))
    base = base + jnp.diag(jnp.full((order,), 0.5 * order, jnp.float32))
    return base


def with_ends(entries, own_key, low, high):
    shape = entries.shape
    index_at = [jax.random.randint(jax.random.fold_in(own_key, axis), (), 0, shape[axis]) for axis in range(len(shape))]
    entries = entries.at[tuple(index_at)].set(low)
    longest = shape.index(max(shape))
    index_at[longest] = (index_at[longest] + 1) % shape[longest]
    return entries.at[tuple(index_at)].set(high)


def levels(rng, shape, pieces, least, high):
    factor_of, own = 1.0, jax.random.fold_in(rng, 6)
    for dim, parts in pieces:
        steps = jnp.exp(jax.random.uniform(jax.random.fold_in(own, dim), (parts,), jnp.float32, least / len(pieces), high / len(pieces)))
        factor_of = factor_of * jnp.repeat(steps, shape[dim] // parts).reshape([-1 if axis == dim else 1 for axis in range(len(shape))])
    return factor_of


def scatter_about(own_key, extent, width, limit, cuts=(), dtype=jnp.bfloat16):
    values = width * jax.random.normal(own_key, extent, jnp.float32)
    if cuts:
        values = values * levels(own_key, extent, cuts, -0.22, 0.18)
    return jnp.clip(values, -limit, limit).astype(dtype)


def setup_inputs(seed: int = 0) -> dict:
    seeds = jax.random.split(jax.random.key(seed), 5)
    ancestor = draw_ancestor(jax.random.fold_in(seeds[4], 71), 0)
    factor = scatter_about(seeds[1], (SN, ORDER, WIDTH), (2.0 / ORDER), 0.0009765625, ((1, 4),))
    inverse_diag = scatter_about(seeds[2], (SN, WIDTH, WIDTH), 1.0, 6.0)
    block_mask = with_ends((jax.random.randint(seeds[3], (SN, NB), 0, 2) < 1).astype(jnp.int32), jax.random.fold_in(seeds[3], 1), 0, 1)
    return dict(ancestor=ancestor, factor=factor, inverse_diag=inverse_diag, block_mask=block_mask)


def reference(ancestor, factor, inverse_diag, block_mask):
    row_mask = jnp.repeat(block_mask, WIDTH, axis=1).astype(jnp.float32)
    blocks = []
    diagonals = []
    for supernode in range(SN):
        masked = factor[supernode].astype(jnp.float32) * row_mask[supernode][:, None]
        product = jnp.dot(ancestor, masked, precision=lax.Precision.HIGHEST, preferred_element_type=jnp.float32)
        column = -row_mask[supernode][:, None] * product
        inner = jnp.dot(masked.T, column, precision=lax.Precision.HIGHEST, preferred_element_type=jnp.float32)
        blocks.append(column)
        diagonals.append(inverse_diag[supernode].astype(jnp.float32) - inner)
    return jnp.stack(blocks, 0), jnp.stack(diagonals, 0)
```

```python
import jax
import jax.numpy as jnp
from jax import lax
from jax.experimental import pallas as pl
from jax.experimental.pallas import tpu as pltpu
from jax.sharding import PartitionSpec as P

WIDTH = 256


def split(x):
    high = lax.reduce_precision(x, 8, 7)
    low = x - high
    return high.astype(jnp.bfloat16), low.astype(jnp.bfloat16)


def dot(a, b):
    return jnp.dot(a, b, preferred_element_type=jnp.float32)


MESH = pl.DeviceIdType.MESH


STEPS = 32.0
BIAS = 4096.0
REACH = 32760.0
HEAD = 16


def part(ref, start, size):
    return ref.at[pl.ds(pl.multiple_of(start, 8), size)]


def encode(value, wire):
    top = jnp.max(jnp.abs(value), axis=0, keepdims=True)
    code = jnp.ceil(jnp.log2(jnp.maximum(top, 1e-30)) * STEPS) + 1.0
    scale = jnp.exp2(code * (-1.0 / STEPS)) * REACH
    number = (code + BIAS).astype(jnp.int32)
    place = lax.broadcasted_iota(jnp.int32, (HEAD, value.shape[1]), 0)
    bits = lax.shift_right_logical(jnp.broadcast_to(number, place.shape), place) & 1
    head = jnp.round(value[:HEAD] * (scale * 0.5)).astype(jnp.int32) * 2 + bits
    rest = jnp.round(value[HEAD:] * scale).astype(jnp.int32)
    wire[...] = jnp.concatenate([head, rest], axis=0).astype(jnp.int16)


def decode(wire):
    value = wire[...].astype(jnp.int32)
    head = value[:HEAD]
    bits = head & 1
    place = lax.broadcasted_iota(jnp.int32, head.shape, 0)
    number = jnp.sum(lax.shift_left(bits, place).astype(jnp.float32), axis=0, keepdims=True)
    scale = jnp.exp2((number - BIAS) * (1.0 / STEPS)) * (1.0 / REACH)
    return jnp.concatenate([head - bits, value[HEAD:]], axis=0).astype(jnp.float32) * scale


def chunk_of(position, deep):
    across = lax.rem(position + deep, 2)
    along = lax.rem(lax.div(position, 2) + lax.div(deep, 2), 2)
    return 2 * lax.rem(across + along, 2) + along


def position_of(chunk, deep):
    along = lax.rem(chunk, 2)
    across = lax.rem(lax.div(chunk, 2) + along, 2)
    return lax.rem(across + deep, 2) + 2 * lax.rem(along + lax.div(deep, 2), 2)


LANES = 128


def remote(source, target, sems, piece, number, device):
    return pltpu.make_async_remote_copy(
        source,
        target,
        sems.at[0, piece, number],
        sems.at[1, piece, number],
        device_id=device,
        device_id_type=MESH,
    )


def fused_kernel(
    factor,
    mask,
    ancestor,
    out,
    gathered,
    turned,
    tiles,
    parts,
    first_out,
    first,
    second_out,
    second,
    ended,
    landing,
    term,
    plane_out,
    plane,
    line,
    shared,
    loads,
    sems,
    plane_sems,
    line_sems,
    shared_sems,
):
    n_rows = lax.axis_size("prow")
    n_cols = lax.axis_size("pcol")
    n_deep = n_cols // 2
    row = lax.axis_index("prow")
    column = lax.axis_index("pcol")
    count, rows_here, width = factor.shape
    slab = out.shape[1]
    lanes_each = slab // LANES
    pieces = count * lanes_each
    half = width // 2
    flip_x = row + 1 - 2 * lax.rem(row, 2)
    flip_y = lax.rem(row + 2, 4)
    flip_both = 3 - row
    x_peer, y_peer = (flip_x, column), (flip_y, column)
    deep, core = lax.div(column, 2), lax.rem(column, 2)
    place = column * n_rows + chunk_of(row, deep)
    target = (lax.div(place, n_cols), lax.rem(place, n_cols))
    here = row * n_cols + column
    from_column = lax.div(here, n_rows)
    origin = (position_of(lax.rem(here, n_rows), lax.div(from_column, 2)), from_column)
    order = (flip_both, flip_x, flip_y, row)
    upper, lower = pl.ds(0, half), pl.ds(half, half)
    group = 2 * n_rows
    member = row * 2 + core
    height = width // group

    def load(t):
        start = pl.multiple_of(chunk_of(order[t % 4], deep) * slab + (t // 4) * LANES, LANES)
        return pltpu.make_async_copy(ancestor.at[:, pl.ds(start, LANES)], tiles.at[t], loads.at[t])

    for t in range(4 * lanes_each):
        load(t).start()

    def in_plane(d):
        peer = lax.rem(member + d, group)
        return peer, (lax.div(peer, 2), deep * 2 + lax.rem(peer, 2))

    def on_line(d):
        peer = lax.rem(deep + d, n_deep)
        return (row, peer * 2 + core)

    barrier = pltpu.get_barrier_semaphore()
    peers = [in_plane(d)[1] for d in range(1, group)] + [on_line(d) for d in range(1, n_deep)]
    for peer in peers:
        pl.semaphore_signal(barrier, inc=1, device_id=peer, device_id_type=MESH)

    @pl.when(place != here)
    def _():
        pl.semaphore_signal(barrier, inc=1, device_id=origin, device_id_type=MESH)

    def turn(k):
        for i in range(0, rows_here, WIDTH):
            block = factor[k, pl.ds(i, WIDTH)].T.astype(jnp.float32) * mask[pl.ds(k, 1), pl.ds(i, WIDTH)]
            turned[pl.ds(k * width, width), pl.ds(i, WIDTH)] = block.astype(jnp.bfloat16)

    turn(0)

    @pl.when(place != here)
    def _():
        pl.semaphore_wait(barrier, len(peers) + 1)

    @pl.when(place == here)
    def _():
        pl.semaphore_wait(barrier, len(peers))

    def early(i, s):
        return remote(first_out.at[i, s], first.at[i, s], sems, i, s, (x_peer, x_peer, y_peer, y_peer)[s])

    def late(i, s):
        return remote(second_out.at[i, s], second.at[i, s], sems, i, 4 + s, (y_peer, x_peer)[s])

    def final(i):
        return remote(ended.at[i], landing.at[i], sems, i, 6, target)

    def compute(i):
        k, j = divmod(i, lanes_each)
        for q in range(4):
            t = 4 * j + q
            if k == 0:
                load(t).wait()
            value = tiles[t]
            high = value.astype(jnp.bfloat16)
            low = (value - high.astype(jnp.float32)).astype(jnp.bfloat16)
            both = dot(turned[pl.ds(k * width, width)], jnp.concatenate([high, low], axis=1))
            parts[4 * i + q] = both[:, :LANES] + both[:, LANES:]
            for s in ((0, 2), (1,), (3,), ())[q]:
                encode(parts[4 * i + q, (upper, upper, lower, lower)[s]], first_out.at[i, s])
                early(i, s).start()

    def forward(i):
        early(i, 0).wait_recv()
        encode(parts[4 * i + 2, upper] + decode(first.at[i, 0]), second_out.at[i, 0])
        late(i, 0).start()
        early(i, 2).wait_recv()
        encode(parts[4 * i + 1, lower] + decode(first.at[i, 2]), second_out.at[i, 1])
        late(i, 1).start()

    def end(i):
        early(i, 1).wait_recv()
        early(i, 3).wait_recv()
        late(i, 0).wait_recv()
        late(i, 1).wait_recv()
        ready = parts[4 * i + 3, upper] + decode(first.at[i, 1]) + decode(second.at[i, 0])
        encode(ready, ended.at[i, upper])
        ready = parts[4 * i + 3, lower] + decode(first.at[i, 3]) + decode(second.at[i, 1])
        encode(ready, ended.at[i, lower])

        @pl.when(place != here)
        def _():
            final(i).start()

        @pl.when(place == here)
        def _():
            landing[i] = ended[i]

    def diagonal(k):
        total = 0.0
        for j in range(lanes_each):
            i = k * lanes_each + j

            @pl.when(place != here)
            def _():
                final(i).wait_recv()

            value = jnp.concatenate([decode(landing.at[i, upper]), decode(landing.at[i, lower])], axis=0)
            parts[4 * i] = value
            high = value.astype(jnp.bfloat16)
            low = (value - high.astype(jnp.float32)).astype(jnp.bfloat16)
            lanes = pl.ds(pl.multiple_of(column * slab + j * LANES, LANES), LANES)
            own = turned[pl.ds(k * width, width), lanes]
            total = total + lax.dot_general(
                jnp.concatenate([own, own], axis=1),
                jnp.concatenate([high, low], axis=1),
                (((1,), (1,)), ((), ())),
                preferred_element_type=jnp.float32,
            )
        term[k] = total
        copies = []
        for d in range(1, group):
            peer, device = in_plane(d)
            encode(term[k, pl.ds(pl.multiple_of(peer * height, height), height)], plane_out.at[k, d - 1])
            copy = remote(plane_out.at[k, d - 1], plane.at[k, d - 1], plane_sems, k, d - 1, device)
            copy.start()
            copies.append(copy)
        yield
        total = term[k, pl.ds(pl.multiple_of(member * height, height), height)]
        for d in range(1, group):
            copies[d - 1].wait_recv()
            total = total + decode(plane.at[k, d - 1])
        encode(total, line.at[k, deep])
        sent = copies
        copies = []
        for d in range(1, n_deep):
            copy = remote(line.at[k, deep], line.at[k, deep], line_sems, k, d - 1, on_line(d))
            copy.start()
            copies.append(copy)
        yield
        for copy in copies:
            copy.wait_recv()
        total = decode(line.at[k, 0])
        for d in range(1, n_deep):
            total = total + decode(line.at[k, d])
        encode(total, shared.at[k, member])
        sent = sent + copies
        copies = []
        for d in range(1, group):
            copy = remote(
                shared.at[k, member], shared.at[k, member], shared_sems, k, d - 1, in_plane(d)[1]
            )
            copy.start()
            copies.append(copy)
        yield
        for copy in copies:
            copy.wait_recv()
        for d in range(group):
            gathered[pl.ds(k * width + d * height, height)] = decode(shared.at[k, d])
        for copy in sent + copies:
            copy.wait_send()

    def turn_back(k):
        for j in range(lanes_each):
            out[k, pl.ds(j * LANES, LANES)] = parts[4 * (k * lanes_each + j)].T

    compute(0)
    for k in range(1, count):
        turn(k)
    for i in range(1, pieces):
        compute(i)
        forward(i - 1)
        if i >= 2:
            end(i - 2)
    forward(pieces - 1)
    running = [diagonal(k) for k in range(count)]
    for k in range(count - 1):
        next(running[k])
    end(pieces - 2)
    for k in range(count - 1):
        next(running[k])
    end(pieces - 1)
    for k in range(count - 1):
        next(running[k])
        turn_back(k)
    next(running[count - 1])
    turn_back(count - 1)
    for _ in range(2):
        next(running[count - 1])
    for k in range(count):
        next(running[k], None)
    for i in range(pieces):
        @pl.when(place != here)
        def _():
            final(i).wait_send()

        for s in range(4):
            early(i, s).wait_send()
        for s in range(2):
            late(i, s).wait_send()


def fused(factor, mask, ancestor):
    count, depth, width = factor.shape
    n_rows, n_cols = lax.axis_size("prow"), lax.axis_size("pcol")
    slab = ancestor.shape[1] // n_rows
    lanes_each = slab // LANES
    pieces = count * lanes_each
    half = width // 2
    group, n_deep = 2 * n_rows, n_cols // 2
    height = width // group
    vmem = pl.BlockSpec(memory_space=pltpu.VMEM)
    f32, i16 = jnp.float32, jnp.int16
    return pl.pallas_call(
        fused_kernel,
        out_shape=(
            jax.ShapeDtypeStruct((count, slab, width), f32),
            jax.ShapeDtypeStruct((count * width, width), f32),
        ),
        in_specs=[vmem, vmem, pl.BlockSpec(memory_space=pl.ANY)],
        out_specs=(vmem, vmem),
        scratch_shapes=[
            pltpu.VMEM((count * width, depth), jnp.bfloat16),
            pltpu.VMEM((4 * lanes_each, depth, LANES), f32),
            pltpu.VMEM((4 * pieces, width, LANES), f32),
            pltpu.VMEM((pieces, 4, half, LANES), i16),
            pltpu.VMEM((pieces, 4, half, LANES), i16),
            pltpu.VMEM((pieces, 2, half, LANES), i16),
            pltpu.VMEM((pieces, 2, half, LANES), i16),
            pltpu.VMEM((pieces, width, LANES), i16),
            pltpu.VMEM((pieces, width, LANES), i16),
            pltpu.VMEM((count, width, width), f32),
            pltpu.VMEM((count, group - 1, height, width), i16),
            pltpu.VMEM((count, group - 1, height, width), i16),
            pltpu.VMEM((count, n_deep, height, width), i16),
            pltpu.VMEM((count, group, height, width), i16),
            pltpu.SemaphoreType.DMA((4 * lanes_each,)),
            pltpu.SemaphoreType.DMA((2, pieces, 7)),
            pltpu.SemaphoreType.DMA((2, count, group - 1)),
            pltpu.SemaphoreType.DMA((2, count, n_deep - 1)),
            pltpu.SemaphoreType.DMA((2, count, group - 1)),
        ],
        compiler_params=pltpu.CompilerParams(
            collective_id=1, has_side_effects=True, vmem_limit_bytes=56 * 1024 * 1024
        ),
    )(factor, mask, ancestor)


def product_plain(turned, ancestor):
    n_rows = lax.axis_size("prow")
    n_cols = lax.axis_size("pcol")
    high, low = split(ancestor)
    partial = dot(turned, high) + dot(turned, low)
    summed = lax.psum_scatter(partial, "prow", scatter_dimension=1, tiled=True)
    pairs = [(r * n_cols + c, c * n_rows + r) for r in range(n_rows) for c in range(n_cols)]
    return lax.ppermute(summed, ("prow", "pcol"), pairs)


def shards(ancestor, factor, inverse_diag, block_mask):
    rows_here = ancestor.shape[0]
    count, _, width = factor.shape
    n_rows = lax.axis_size("prow")
    n_cols = lax.axis_size("pcol")
    column = lax.axis_index("pcol")
    grid_row = lax.axis_index("prow")
    slab = rows_here // n_cols
    row_mask = jnp.repeat(block_mask, WIDTH, axis=1).astype(jnp.float32)
    own_mask = lax.dynamic_slice_in_dim(row_mask, grid_row * rows_here, rows_here, 1)
    slab_mask = lax.dynamic_slice_in_dim(own_mask, column * slab, slab, 1)
    inverse = inverse_diag.astype(jnp.float32)
    fits = n_rows == 4 and n_cols % 2 == 0 and n_cols > 2 and width == WIDTH
    fits = fits and slab % LANES == 0 and slab * n_rows == ancestor.shape[1]
    if fits:
        placed, total = fused(factor, own_mask, ancestor)
        return (-slab_mask[:, :, None] * placed, inverse + total.reshape(inverse.shape))
    masked = factor * own_mask[:, :, None].astype(factor.dtype)
    turned = masked.transpose(0, 2, 1).reshape(count * width, rows_here)
    placed = product_plain(turned, ancestor).reshape(count, width, slab)
    column_block = -slab_mask[:, :, None] * placed.transpose(0, 2, 1)
    own_slab = lax.dynamic_slice_in_dim(masked, column * slab, slab, 1)
    high, low = split(column_block)
    term = jnp.stack([dot(own_slab[k].T, high[k]) + dot(own_slab[k].T, low[k]) for k in range(count)])
    return (column_block, inverse - lax.psum(term, ("prow", "pcol")))


def solution(mesh):
    return jax.shard_map(
        shards,
        mesh=mesh,
        in_specs=(P("prow", "pcol"), P(None, "prow", None), P(), P()),
        out_specs=(P(None, ("prow", "pcol"), None), P()),
        check_vma=False,
    )
```

```python
import jax
import jax.numpy as jnp
from jax import lax
from jax.experimental import pallas as pl
from jax.experimental.pallas import tpu as pltpu
from jax.sharding import PartitionSpec as P

WIDTH = 256


def split(x):
    high = lax.reduce_precision(x, 8, 7)
    low = x - high
    return high.astype(jnp.bfloat16), low.astype(jnp.bfloat16)


def dot(a, b):
    return jnp.dot(a, b, preferred_element_type=jnp.float32)


MESH = pl.DeviceIdType.MESH


STEPS = 32.0
BIAS = 4096.0
REACH = 32760.0
HEAD = 16


def part(ref, start, size):
    return ref.at[pl.ds(pl.multiple_of(start, 8), size)]


def encode(value, wire):
    top = jnp.max(jnp.abs(value), axis=0, keepdims=True)
    code = jnp.ceil(jnp.log2(jnp.maximum(top, 1e-30)) * STEPS) + 1.0
    scale = jnp.exp2(code * (-1.0 / STEPS)) * REACH
    number = (code + BIAS).astype(jnp.int32)
    place = lax.broadcasted_iota(jnp.int32, (HEAD, value.shape[1]), 0)
    bits = lax.shift_right_logical(jnp.broadcast_to(number, place.shape), place) & 1
    head = jnp.round(value[:HEAD] * (scale * 0.5)).astype(jnp.int32) * 2 + bits
    rest = jnp.round(value[HEAD:] * scale).astype(jnp.int32)
    wire[...] = jnp.concatenate([head, rest], axis=0).astype(jnp.int16)


def decode(wire):
    value = wire[...].astype(jnp.int32)
    head = value[:HEAD]
    bits = head & 1
    place = lax.broadcasted_iota(jnp.int32, head.shape, 0)
    number = jnp.sum(lax.shift_left(bits, place).astype(jnp.float32), axis=0, keepdims=True)
    scale = jnp.exp2((number - BIAS) * (1.0 / STEPS)) * (1.0 / REACH)
    return jnp.concatenate([head - bits, value[HEAD:]], axis=0).astype(jnp.float32) * scale


def chunk_of(position, deep):
    across = lax.rem(position + deep, 2)
    along = lax.rem(lax.div(position, 2) + lax.div(deep, 2), 2)
    return 2 * lax.rem(across + along, 2) + along


def position_of(chunk, deep):
    along = lax.rem(chunk, 2)
    across = lax.rem(lax.div(chunk, 2) + along, 2)
    return lax.rem(across + deep, 2) + 2 * lax.rem(along + lax.div(deep, 2), 2)


LANES = 128


def remote(source, target, sems, piece, number, device):
    return pltpu.make_async_remote_copy(
        source,
        target,
        sems.at[0, piece, number],
        sems.at[1, piece, number],
        device_id=device,
        device_id_type=MESH,
    )


def fused_kernel(
    factor,
    mask,
    ancestor,
    out,
    gathered,
    turned,
    tiles,
    parts,
    first_out,
    first,
    second_out,
    second,
    ended,
    landing,
    term,
    plane_out,
    plane,
    line,
    shared,
    loads,
    sems,
    plane_sems,
    line_sems,
    shared_sems,
):
    n_rows = lax.axis_size("prow")
    n_cols = lax.axis_size("pcol")
    n_deep = n_cols // 2
    row = lax.axis_index("prow")
    column = lax.axis_index("pcol")
    count, rows_here, width = factor.shape
    slab = out.shape[1]
    lanes_each = slab // LANES
    pieces = count * lanes_each
    half = width // 2
    flip_x = row + 1 - 2 * lax.rem(row, 2)
    flip_y = lax.rem(row + 2, 4)
    flip_both = 3 - row
    x_peer, y_peer = (flip_x, column), (flip_y, column)
    deep, core = lax.div(column, 2), lax.rem(column, 2)
    place = column * n_rows + chunk_of(row, deep)
    target = (lax.div(place, n_cols), lax.rem(place, n_cols))
    here = row * n_cols + column
    from_column = lax.div(here, n_rows)
    origin = (position_of(lax.rem(here, n_rows), lax.div(from_column, 2)), from_column)
    order = (flip_both, flip_x, flip_y, row)
    upper, lower = pl.ds(0, half), pl.ds(half, half)
    group = 2 * n_rows
    member = row * 2 + core
    height = width // group

    def load(t):
        start = pl.multiple_of(chunk_of(order[t % 4], deep) * slab + (t // 4) * LANES, LANES)
        return pltpu.make_async_copy(ancestor.at[:, pl.ds(start, LANES)], tiles.at[t], loads.at[t])

    for t in range(4 * lanes_each):
        load(t).start()

    def in_plane(d):
        peer = lax.rem(member + d, group)
        return peer, (lax.div(peer, 2), deep * 2 + lax.rem(peer, 2))

    def on_line(d):
        peer = lax.rem(deep + d, n_deep)
        return (row, peer * 2 + core)

    barrier = pltpu.get_barrier_semaphore()
    peers = [in_plane(d)[1] for d in range(1, group)] + [on_line(d) for d in range(1, n_deep)]
    for peer in peers:
        pl.semaphore_signal(barrier, inc=1, device_id=peer, device_id_type=MESH)

    @pl.when(place != here)
    def _():
        pl.semaphore_signal(barrier, inc=1, device_id=origin, device_id_type=MESH)

    def turn(k):
        for i in range(0, rows_here, WIDTH):
            block = factor[k, pl.ds(i, WIDTH)].T.astype(jnp.float32) * mask[pl.ds(k, 1), pl.ds(i, WIDTH)]
            turned[pl.ds(k * width, width), pl.ds(i, WIDTH)] = block.astype(jnp.bfloat16)

    turn(0)

    @pl.when(place != here)
    def _():
        pl.semaphore_wait(barrier, len(peers) + 1)

    @pl.when(place == here)
    def _():
        pl.semaphore_wait(barrier, len(peers))

    def early(i, s):
        return remote(first_out.at[i, s], first.at[i, s], sems, i, s, (x_peer, x_peer, y_peer, y_peer)[s])

    def late(i, s):
        return remote(second_out.at[i, s], second.at[i, s], sems, i, 4 + s, (y_peer, x_peer)[s])

    def final(i):
        return remote(ended.at[i], landing.at[i], sems, i, 6, target)

    def compute(i):
        k, j = divmod(i, lanes_each)
        for q in range(4):
            t = 4 * j + q
            if k == 0:
                load(t).wait()
            value = tiles[t]
            high = value.astype(jnp.bfloat16)
            low = (value - high.astype(jnp.float32)).astype(jnp.bfloat16)
            stacked = jnp.concatenate([high, low], axis=1)
            for h in range(2):
                both = dot(turned[pl.ds(k * width + h * half, half)], stacked)
                parts[4 * i + q, pl.ds(h * half, half)] = both[:, :LANES] + both[:, LANES:]
            for s in ((0, 2), (1,), (3,), ())[q]:
                encode(parts[4 * i + q, (upper, upper, lower, lower)[s]], first_out.at[i, s])
                early(i, s).start()

    def forward(i):
        early(i, 0).wait_recv()
        encode(parts[4 * i + 2, upper] + decode(first.at[i, 0]), second_out.at[i, 0])
        late(i, 0).start()
        early(i, 2).wait_recv()
        encode(parts[4 * i + 1, lower] + decode(first.at[i, 2]), second_out.at[i, 1])
        late(i, 1).start()

    def end(i):
        early(i, 1).wait_recv()
        early(i, 3).wait_recv()
        late(i, 0).wait_recv()
        late(i, 1).wait_recv()
        ready = parts[4 * i + 3, upper] + decode(first.at[i, 1]) + decode(second.at[i, 0])
        encode(ready, ended.at[i, upper])
        ready = parts[4 * i + 3, lower] + decode(first.at[i, 3]) + decode(second.at[i, 1])
        encode(ready, ended.at[i, lower])

        @pl.when(place != here)
        def _():
            final(i).start()

        @pl.when(place == here)
        def _():
            landing[i] = ended[i]

    def diagonal(k):
        total = 0.0
        for j in range(lanes_each):
            i = k * lanes_each + j

            @pl.when(place != here)
            def _():
                final(i).wait_recv()

            value = jnp.concatenate([decode(landing.at[i, upper]), decode(landing.at[i, lower])], axis=0)
            parts[4 * i] = value
            high = value.astype(jnp.bfloat16)
            low = (value - high.astype(jnp.float32)).astype(jnp.bfloat16)
            lanes = pl.ds(pl.multiple_of(column * slab + j * LANES, LANES), LANES)
            own = turned[pl.ds(k * width, width), lanes]
            total = total + lax.dot_general(
                jnp.concatenate([own, own], axis=1),
                jnp.concatenate([high, low], axis=1),
                (((1,), (1,)), ((), ())),
                preferred_element_type=jnp.float32,
            )
        term[k] = total
        copies = []
        for d in range(1, group):
            peer, device = in_plane(d)
            encode(term[k, pl.ds(pl.multiple_of(peer * height, height), height)], plane_out.at[k, d - 1])
            copy = remote(plane_out.at[k, d - 1], plane.at[k, d - 1], plane_sems, k, d - 1, device)
            copy.start()
            copies.append(copy)
        yield
        total = term[k, pl.ds(pl.multiple_of(member * height, height), height)]
        for d in range(1, group):
            copies[d - 1].wait_recv()
            total = total + decode(plane.at[k, d - 1])
        encode(total, line.at[k, deep])
        sent = copies
        copies = []
        for d in range(1, n_deep):
            copy = remote(line.at[k, deep], line.at[k, deep], line_sems, k, d - 1, on_line(d))
            copy.start()
            copies.append(copy)
        yield
        for copy in copies:
            copy.wait_recv()
        total = decode(line.at[k, 0])
        for d in range(1, n_deep):
            total = total + decode(line.at[k, d])
        encode(total, shared.at[k, member])
        sent = sent + copies
        copies = []
        for d in range(1, group):
            copy = remote(
                shared.at[k, member], shared.at[k, member], shared_sems, k, d - 1, in_plane(d)[1]
            )
            copy.start()
            copies.append(copy)
        yield
        for copy in copies:
            copy.wait_recv()
        for d in range(group):
            gathered[pl.ds(k * width + d * height, height)] = decode(shared.at[k, d])
        for copy in sent + copies:
            copy.wait_send()

    def turn_back(k):
        for j in range(lanes_each):
            out[k, pl.ds(j * LANES, LANES)] = parts[4 * (k * lanes_each + j)].T

    compute(0)
    for k in range(1, count):
        turn(k)
    for i in range(1, pieces):
        compute(i)
        forward(i - 1)
        if i >= 2:
            end(i - 2)
    forward(pieces - 1)
    running = [diagonal(k) for k in range(count)]
    for k in range(count - 1):
        next(running[k])
    end(pieces - 2)
    for k in range(count - 1):
        next(running[k])
    end(pieces - 1)
    for k in range(count - 1):
        next(running[k])
        turn_back(k)
    next(running[count - 1])
    turn_back(count - 1)
    for _ in range(2):
        next(running[count - 1])
    for k in range(count):
        next(running[k], None)
    for i in range(pieces):
        @pl.when(place != here)
        def _():
            final(i).wait_send()

        for s in range(4):
            early(i, s).wait_send()
        for s in range(2):
            late(i, s).wait_send()


def fused(factor, mask, ancestor):
    count, depth, width = factor.shape
    n_rows, n_cols = lax.axis_size("prow"), lax.axis_size("pcol")
    slab = ancestor.shape[1] // n_rows
    lanes_each = slab // LANES
    pieces = count * lanes_each
    half = width // 2
    group, n_deep = 2 * n_rows, n_cols // 2
    height = width // group
    vmem = pl.BlockSpec(memory_space=pltpu.VMEM)
    f32, i16 = jnp.float32, jnp.int16
    return pl.pallas_call(
        fused_kernel,
        out_shape=(
            jax.ShapeDtypeStruct((count, slab, width), f32),
            jax.ShapeDtypeStruct((count * width, width), f32),
        ),
        in_specs=[vmem, vmem, pl.BlockSpec(memory_space=pl.ANY)],
        out_specs=(vmem, vmem),
        scratch_shapes=[
            pltpu.VMEM((count * width, depth), jnp.bfloat16),
            pltpu.VMEM((4 * lanes_each, depth, LANES), f32),
            pltpu.VMEM((4 * pieces, width, LANES), f32),
            pltpu.VMEM((pieces, 4, half, LANES), i16),
            pltpu.VMEM((pieces, 4, half, LANES), i16),
            pltpu.VMEM((pieces, 2, half, LANES), i16),
            pltpu.VMEM((pieces, 2, half, LANES), i16),
            pltpu.VMEM((pieces, width, LANES), i16),
            pltpu.VMEM((pieces, width, LANES), i16),
            pltpu.VMEM((count, width, width), f32),
            pltpu.VMEM((count, group - 1, height, width), i16),
            pltpu.VMEM((count, group - 1, height, width), i16),
            pltpu.VMEM((count, n_deep, height, width), i16),
            pltpu.VMEM((count, group, height, width), i16),
            pltpu.SemaphoreType.DMA((4 * lanes_each,)),
            pltpu.SemaphoreType.DMA((2, pieces, 7)),
            pltpu.SemaphoreType.DMA((2, count, group - 1)),
            pltpu.SemaphoreType.DMA((2, count, n_deep - 1)),
            pltpu.SemaphoreType.DMA((2, count, group - 1)),
        ],
        compiler_params=pltpu.CompilerParams(
            collective_id=1, has_side_effects=True, vmem_limit_bytes=56 * 1024 * 1024
        ),
    )(factor, mask, ancestor)


def product_plain(turned, ancestor):
    n_rows = lax.axis_size("prow")
    n_cols = lax.axis_size("pcol")
    high, low = split(ancestor)
    partial = dot(turned, high) + dot(turned, low)
    summed = lax.psum_scatter(partial, "prow", scatter_dimension=1, tiled=True)
    pairs = [(r * n_cols + c, c * n_rows + r) for r in range(n_rows) for c in range(n_cols)]
    return lax.ppermute(summed, ("prow", "pcol"), pairs)


def shards(ancestor, factor, inverse_diag, block_mask):
    rows_here = ancestor.shape[0]
    count, _, width = factor.shape
    n_rows = lax.axis_size("prow")
    n_cols = lax.axis_size("pcol")
    column = lax.axis_index("pcol")
    grid_row = lax.axis_index("prow")
    slab = rows_here // n_cols
    row_mask = jnp.repeat(block_mask, WIDTH, axis=1).astype(jnp.float32)
    own_mask = lax.dynamic_slice_in_dim(row_mask, grid_row * rows_here, rows_here, 1)
    slab_mask = lax.dynamic_slice_in_dim(own_mask, column * slab, slab, 1)
    inverse = inverse_diag.astype(jnp.float32)
    fits = n_rows == 4 and n_cols % 2 == 0 and n_cols > 2 and width == WIDTH
    fits = fits and slab % LANES == 0 and slab * n_rows == ancestor.shape[1]
    if fits:
        placed, total = fused(factor, own_mask, ancestor)
        return (-slab_mask[:, :, None] * placed, inverse + total.reshape(inverse.shape))
    masked = factor * own_mask[:, :, None].astype(factor.dtype)
    turned = masked.transpose(0, 2, 1).reshape(count * width, rows_here)
    placed = product_plain(turned, ancestor).reshape(count, width, slab)
    column_block = -slab_mask[:, :, None] * placed.transpose(0, 2, 1)
    own_slab = lax.dynamic_slice_in_dim(masked, column * slab, slab, 1)
    high, low = split(column_block)
    term = jnp.stack([dot(own_slab[k].T, high[k]) + dot(own_slab[k].T, low[k]) for k in range(count)])
    return (column_block, inverse - lax.psum(term, ("prow", "pcol")))


def solution(mesh):
    return jax.shard_map(
        shards,
        mesh=mesh,
        in_specs=(P("prow", "pcol"), P(None, "prow", None), P(), P()),
        out_specs=(P(None, ("prow", "pcol"), None), P()),
        check_vma=False,
    )
```

```python
import jax
import jax.numpy as jnp
from jax import lax
from jax.experimental import pallas as pl
from jax.experimental.pallas import tpu as pltpu
from jax.sharding import PartitionSpec as P

WIDTH = 256


def split(x):
    high = lax.reduce_precision(x, 8, 7)
    low = x - high
    return high.astype(jnp.bfloat16), low.astype(jnp.bfloat16)


def dot(a, b):
    return jnp.dot(a, b, preferred_element_type=jnp.float32)


MESH = pl.DeviceIdType.MESH


STEPS = 32.0
BIAS = 4096.0
REACH = 32760.0
HEAD = 16


def part(ref, start, size):
    return ref.at[pl.ds(pl.multiple_of(start, 8), size)]


def encode(value, wire):
    top = jnp.max(jnp.abs(value), axis=0, keepdims=True)
    code = jnp.ceil(jnp.log2(jnp.maximum(top, 1e-30)) * STEPS) + 1.0
    scale = jnp.exp2(code * (-1.0 / STEPS)) * REACH
    number = (code + BIAS).astype(jnp.int32)
    place = lax.broadcasted_iota(jnp.int32, (HEAD, value.shape[1]), 0)
    bits = lax.shift_right_logical(jnp.broadcast_to(number, place.shape), place) & 1
    head = jnp.round(value[:HEAD] * (scale * 0.5)).astype(jnp.int32) * 2 + bits
    rest = jnp.round(value[HEAD:] * scale).astype(jnp.int32)
    wire[...] = jnp.concatenate([head, rest], axis=0).astype(jnp.int16)


def decode(wire):
    value = wire[...].astype(jnp.int32)
    head = value[:HEAD]
    bits = head & 1
    place = lax.broadcasted_iota(jnp.int32, head.shape, 0)
    number = jnp.sum(lax.shift_left(bits, place).astype(jnp.float32), axis=0, keepdims=True)
    scale = jnp.exp2((number - BIAS) * (1.0 / STEPS)) * (1.0 / REACH)
    return jnp.concatenate([head - bits, value[HEAD:]], axis=0).astype(jnp.float32) * scale


def chunk_of(position, deep):
    across = lax.rem(position + deep, 2)
    along = lax.rem(lax.div(position, 2) + lax.div(deep, 2), 2)
    return 2 * lax.rem(across + along, 2) + along


def position_of(chunk, deep):
    along = lax.rem(chunk, 2)
    across = lax.rem(lax.div(chunk, 2) + along, 2)
    return lax.rem(across + deep, 2) + 2 * lax.rem(along + lax.div(deep, 2), 2)


LANES = 128
AHEAD = 3


def remote(source, target, sems, piece, number, device):
    return pltpu.make_async_remote_copy(
        source,
        target,
        sems.at[0, piece, number],
        sems.at[1, piece, number],
        device_id=device,
        device_id_type=MESH,
    )


def fused_kernel(
    factor_hbm,
    mask,
    ancestor,
    out,
    gathered,
    factor,
    turned,
    tiles,
    parts,
    first_out,
    first,
    second_out,
    second,
    ended,
    landing,
    term,
    plane_out,
    plane,
    line,
    shared,
    loads,
    sems,
    plane_sems,
    line_sems,
    shared_sems,
    small_loads,
):
    n_rows = lax.axis_size("prow")
    n_cols = lax.axis_size("pcol")
    n_deep = n_cols // 2
    row = lax.axis_index("prow")
    column = lax.axis_index("pcol")
    count, rows_here, width = factor.shape
    slab = out.shape[1]
    lanes_each = slab // LANES
    pieces = count * lanes_each
    half = width // 2
    flip_x = row + 1 - 2 * lax.rem(row, 2)
    flip_y = lax.rem(row + 2, 4)
    flip_both = 3 - row
    x_peer, y_peer = (flip_x, column), (flip_y, column)
    deep, core = lax.div(column, 2), lax.rem(column, 2)
    place = column * n_rows + chunk_of(row, deep)
    target = (lax.div(place, n_cols), lax.rem(place, n_cols))
    here = row * n_cols + column
    from_column = lax.div(here, n_rows)
    origin = (position_of(lax.rem(here, n_rows), lax.div(from_column, 2)), from_column)
    order = (flip_both, flip_x, flip_y, row)
    upper, lower = pl.ds(0, half), pl.ds(half, half)
    group = 2 * n_rows
    member = row * 2 + core
    height = 3 * width // (2 * group)

    def load(t):
        start = pl.multiple_of(chunk_of(order[t % 4], deep) * slab + (t // 4) * LANES, LANES)
        return pltpu.make_async_copy(ancestor.at[:, pl.ds(start, LANES)], tiles.at[t], loads.at[t])

    def load_factor(k):
        return pltpu.make_async_copy(factor_hbm.at[k], factor.at[k], small_loads.at[k])

    load_factor(0).start()
    for t in range(AHEAD):
        load(t).start()
    blocks_here = rows_here // WIDTH

    def in_plane(d):
        peer = lax.rem(member + d, group)
        return peer, (lax.div(peer, 2), deep * 2 + lax.rem(peer, 2))

    def on_line(d):
        peer = lax.rem(deep + d, n_deep)
        return (row, peer * 2 + core)

    barrier = pltpu.get_barrier_semaphore()
    peers = [in_plane(d)[1] for d in range(1, group)] + [on_line(d) for d in range(1, n_deep)]
    for peer in peers:
        pl.semaphore_signal(barrier, inc=1, device_id=peer, device_id_type=MESH)

    @pl.when(place != here)
    def _():
        pl.semaphore_signal(barrier, inc=1, device_id=origin, device_id_type=MESH)

    def turn(k):
        load_factor(k).wait()
        for i in range(blocks_here):
            at = pl.ds(i * WIDTH, WIDTH)
            kept = mask[k, row * blocks_here + i].astype(jnp.float32)
            block = factor[k, at].T.astype(jnp.float32) * kept
            turned[pl.ds(k * width, width), at] = block.astype(jnp.bfloat16)

    turn(0)

    @pl.when(place != here)
    def _():
        pl.semaphore_wait(barrier, len(peers) + 1)

    @pl.when(place == here)
    def _():
        pl.semaphore_wait(barrier, len(peers))

    def early(i, s):
        return remote(first_out.at[i, s], first.at[i, s], sems, i, s, (x_peer, x_peer, y_peer, y_peer)[s])

    def late(i, s):
        return remote(second_out.at[i, s], second.at[i, s], sems, i, 4 + s, (y_peer, x_peer)[s])

    def final(i):
        return remote(ended.at[i], landing.at[i], sems, i, 6, target)

    def compute(i):
        k, j = divmod(i, lanes_each)
        for q in range(4):
            t = 4 * j + q
            if k == 0:
                load(t).wait()
                if t + AHEAD < 4 * lanes_each:
                    load(t + AHEAD).start()
                if t == 2:
                    for other in range(1, count):
                        load_factor(other).start()
            value = tiles[t]
            high = value.astype(jnp.bfloat16)
            low = (value - high.astype(jnp.float32)).astype(jnp.bfloat16)
            stacked = jnp.concatenate([high, low], axis=1)
            for h in range(2):
                both = dot(turned[pl.ds(k * width + h * half, half)], stacked)
                parts[4 * i + q, pl.ds(h * half, half)] = both[:, :LANES] + both[:, LANES:]
            for s in ((0, 2), (1,), (3,), ())[q]:
                encode(parts[4 * i + q, (upper, upper, lower, lower)[s]], first_out.at[i, s])
                early(i, s).start()

    def forward(i):
        early(i, 0).wait_recv()
        encode(parts[4 * i + 2, upper] + decode(first.at[i, 0]), second_out.at[i, 0])
        late(i, 0).start()
        early(i, 2).wait_recv()
        encode(parts[4 * i + 1, lower] + decode(first.at[i, 2]), second_out.at[i, 1])
        late(i, 1).start()

    def end(i):
        early(i, 1).wait_recv()
        early(i, 3).wait_recv()
        late(i, 0).wait_recv()
        late(i, 1).wait_recv()
        ready = parts[4 * i + 3, upper] + decode(first.at[i, 1]) + decode(second.at[i, 0])
        encode(ready, ended.at[i, upper])
        ready = parts[4 * i + 3, lower] + decode(first.at[i, 3]) + decode(second.at[i, 1])
        encode(ready, ended.at[i, lower])

        @pl.when(place != here)
        def _():
            final(i).start()

        @pl.when(place == here)
        def _():
            landing[i] = ended[i]

    def diagonal(k):
        total = 0.0
        for j in range(lanes_each):
            i = k * lanes_each + j

            @pl.when(place != here)
            def _():
                final(i).wait_recv()

            value = jnp.concatenate([decode(landing.at[i, upper]), decode(landing.at[i, lower])], axis=0)
            parts[4 * i] = value
            high = value.astype(jnp.bfloat16)
            low = (value - high.astype(jnp.float32)).astype(jnp.bfloat16)
            lanes = pl.ds(pl.multiple_of(column * slab + j * LANES, LANES), LANES)
            own = turned[pl.ds(k * width, width), lanes]
            total = total + lax.dot_general(
                jnp.concatenate([own, own], axis=1),
                jnp.concatenate([high, low], axis=1),
                (((1,), (1,)), ((), ())),
                preferred_element_type=jnp.float32,
            )
        mid = width // 2
        term[k, pl.ds(0, mid)] = total[:mid, :mid]
        term[k, pl.ds(mid, mid)] = total[:mid, mid:]
        term[k, pl.ds(2 * mid, mid)] = total[mid:, mid:]
        copies = []
        for d in range(1, group):
            peer, device = in_plane(d)
            encode(term[k, pl.ds(pl.multiple_of(peer * height, height), height)], plane_out.at[k, d - 1])
            copy = remote(plane_out.at[k, d - 1], plane.at[k, d - 1], plane_sems, k, d - 1, device)
            copy.start()
            copies.append(copy)
        yield
        total = term[k, pl.ds(pl.multiple_of(member * height, height), height)]
        for d in range(1, group):
            copies[d - 1].wait_recv()
            total = total + decode(plane.at[k, d - 1])
        encode(total, line.at[k, deep])
        sent = copies
        copies = []
        for d in range(1, n_deep):
            copy = remote(line.at[k, deep], line.at[k, deep], line_sems, k, d - 1, on_line(d))
            copy.start()
            copies.append(copy)
        yield
        for copy in copies:
            copy.wait_recv()
        total = decode(line.at[k, 0])
        for d in range(1, n_deep):
            total = total + decode(line.at[k, d])
        encode(total, shared.at[k, member])
        sent = sent + copies
        copies = []
        for d in range(1, group):
            copy = remote(
                shared.at[k, member], shared.at[k, member], shared_sems, k, d - 1, in_plane(d)[1]
            )
            copy.start()
            copies.append(copy)
        yield
        for copy in copies:
            copy.wait_recv()
        for d in range(group):
            term[k, pl.ds(d * height, height)] = decode(shared.at[k, d])
        cross = term[k, pl.ds(mid, mid)]
        top = jnp.concatenate([term[k, pl.ds(0, mid)], cross], axis=1)
        bottom = jnp.concatenate([cross.T, term[k, pl.ds(2 * mid, mid)]], axis=1)
        gathered[k] = jnp.concatenate([top, bottom], axis=0)
        for copy in sent + copies:
            copy.wait_send()

    def turn_back(k):
        for j in range(lanes_each):
            start = row * rows_here + column * slab + j * LANES
            kept = mask[k, lax.div(start, WIDTH)].astype(jnp.float32)
            out[k, pl.ds(j * LANES, LANES)] = parts[4 * (k * lanes_each + j)].T * kept

    for i in range(pieces):
        compute(i)
        if i == 0:
            for k in range(1, count):
                turn(k)
        if i >= 1:
            forward(i - 1)
        if i >= 2:
            end(i - 2)
    forward(pieces - 1)
    end(pieces - 2)
    running = [diagonal(k) for k in range(count)]
    for k in range(count - 1):
        next(running[k])
    end(pieces - 1)
    for k in range(count - 1):
        next(running[k])
    next(running[count - 1])
    for k in range(count - 1):
        next(running[k])
        turn_back(k)
    next(running[count - 1])
    turn_back(count - 1)
    next(running[count - 1])
    for k in range(count):
        next(running[k], None)
    for i in range(pieces):
        @pl.when(place != here)
        def _():
            final(i).wait_send()

        for s in range(4):
            early(i, s).wait_send()
        for s in range(2):
            late(i, s).wait_send()


def fused(factor, mask, ancestor):
    count, depth, width = factor.shape
    n_rows, n_cols = lax.axis_size("prow"), lax.axis_size("pcol")
    slab = ancestor.shape[1] // n_rows
    lanes_each = slab // LANES
    pieces = count * lanes_each
    half = width // 2
    group, n_deep = 2 * n_rows, n_cols // 2
    height = 3 * width // (2 * group)
    vmem, hbm = pl.BlockSpec(memory_space=pltpu.VMEM), pl.BlockSpec(memory_space=pl.ANY)
    f32, i16 = jnp.float32, jnp.int16
    return pl.pallas_call(
        fused_kernel,
        out_shape=(
            jax.ShapeDtypeStruct((count, slab, width), f32),
            jax.ShapeDtypeStruct((count, width, width), f32),
        ),
        in_specs=[hbm, pl.BlockSpec(memory_space=pltpu.SMEM), hbm],
        out_specs=(vmem, vmem),
        scratch_shapes=[
            pltpu.VMEM(factor.shape, factor.dtype),
            pltpu.VMEM((count * width, depth), jnp.bfloat16),
            pltpu.VMEM((4 * lanes_each, depth, LANES), f32),
            pltpu.VMEM((4 * pieces, width, LANES), f32),
            pltpu.VMEM((pieces, 4, half, LANES), i16),
            pltpu.VMEM((pieces, 4, half, LANES), i16),
            pltpu.VMEM((pieces, 2, half, LANES), i16),
            pltpu.VMEM((pieces, 2, half, LANES), i16),
            pltpu.VMEM((pieces, width, LANES), i16),
            pltpu.VMEM((pieces, width, LANES), i16),
            pltpu.VMEM((count, group * height, width // 2), f32),
            pltpu.VMEM((count, group - 1, height, width // 2), i16),
            pltpu.VMEM((count, group - 1, height, width // 2), i16),
            pltpu.VMEM((count, n_deep, height, width // 2), i16),
            pltpu.VMEM((count, group, height, width // 2), i16),
            pltpu.SemaphoreType.DMA((4 * lanes_each,)),
            pltpu.SemaphoreType.DMA((2, pieces, 7)),
            pltpu.SemaphoreType.DMA((2, count, group - 1)),
            pltpu.SemaphoreType.DMA((2, count, n_deep - 1)),
            pltpu.SemaphoreType.DMA((2, count, group - 1)),
            pltpu.SemaphoreType.DMA((count,)),
        ],
        compiler_params=pltpu.CompilerParams(
            collective_id=1, has_side_effects=True, vmem_limit_bytes=50 * 1024 * 1024
        ),
    )(factor, mask, ancestor)


def product_plain(turned, ancestor):
    n_rows = lax.axis_size("prow")
    n_cols = lax.axis_size("pcol")
    high, low = split(ancestor)
    partial = dot(turned, high) + dot(turned, low)
    summed = lax.psum_scatter(partial, "prow", scatter_dimension=1, tiled=True)
    pairs = [(r * n_cols + c, c * n_rows + r) for r in range(n_rows) for c in range(n_cols)]
    return lax.ppermute(summed, ("prow", "pcol"), pairs)


def shards(ancestor, factor, inverse_diag, block_mask):
    rows_here = ancestor.shape[0]
    count, _, width = factor.shape
    n_rows = lax.axis_size("prow")
    n_cols = lax.axis_size("pcol")
    column = lax.axis_index("pcol")
    grid_row = lax.axis_index("prow")
    slab = rows_here // n_cols
    fits = n_rows == 4 and n_cols % 2 == 0 and n_cols > 2 and width == WIDTH
    fits = fits and slab % LANES == 0 and slab * n_rows == ancestor.shape[1]
    if fits:
        placed, total = fused(factor, block_mask, ancestor)
        return (-placed, inverse_diag.astype(jnp.float32) + total)
    row_mask = jnp.repeat(block_mask, WIDTH, axis=1).astype(jnp.float32)
    own_mask = lax.dynamic_slice_in_dim(row_mask, grid_row * rows_here, rows_here, 1)
    slab_mask = lax.dynamic_slice_in_dim(own_mask, column * slab, slab, 1)
    inverse = inverse_diag.astype(jnp.float32)
    masked = factor * own_mask[:, :, None].astype(factor.dtype)
    turned = masked.transpose(0, 2, 1).reshape(count * width, rows_here)
    placed = product_plain(turned, ancestor).reshape(count, width, slab)
    column_block = -slab_mask[:, :, None] * placed.transpose(0, 2, 1)
    own_slab = lax.dynamic_slice_in_dim(masked, column * slab, slab, 1)
    high, low = split(column_block)
    term = jnp.stack([dot(own_slab[k].T, high[k]) + dot(own_slab[k].T, low[k]) for k in range(count)])
    return (column_block, inverse - lax.psum(term, ("prow", "pcol")))


def solution(mesh):
    return jax.shard_map(
        shards,
        mesh=mesh,
        in_specs=(P("prow", "pcol"), P(None, "prow", None), P(), P()),
        out_specs=(P(None, ("prow", "pcol"), None), P()),
        check_vma=False,
    )
```

```python
import jax
import jax.numpy as jnp
from jax import lax
from jax.experimental import pallas as pl
from jax.experimental.pallas import tpu as pltpu
from jax.sharding import PartitionSpec as P

WIDTH = 256


def split(x):
    high = lax.reduce_precision(x, 8, 7)
    low = x - high
    return high.astype(jnp.bfloat16), low.astype(jnp.bfloat16)


def dot(a, b):
    return jnp.dot(a, b, preferred_element_type=jnp.float32)


MESH = pl.DeviceIdType.MESH


STEPS = 32.0
BIAS = 4096.0
REACH = 32760.0
HEAD = 16


def part(ref, start, size):
    return ref.at[pl.ds(pl.multiple_of(start, 8), size)]


def encode(value, wire):
    top = jnp.max(jnp.abs(value), axis=0, keepdims=True)
    code = jnp.ceil(jnp.log2(jnp.maximum(top, 1e-30)) * STEPS) + 1.0
    scale = jnp.exp2(code * (-1.0 / STEPS)) * REACH
    number = (code + BIAS).astype(jnp.int32)
    place = lax.broadcasted_iota(jnp.int32, (HEAD, value.shape[1]), 0)
    bits = lax.shift_right_logical(jnp.broadcast_to(number, place.shape), place) & 1
    head = jnp.round(value[:HEAD] * (scale * 0.5)).astype(jnp.int32) * 2 + bits
    rest = jnp.round(value[HEAD:] * scale).astype(jnp.int32)
    wire[...] = jnp.concatenate([head, rest], axis=0).astype(jnp.int16)


def decode(wire):
    value = wire[...].astype(jnp.int32)
    head = value[:HEAD]
    bits = head & 1
    place = lax.broadcasted_iota(jnp.int32, head.shape, 0)
    number = jnp.sum(lax.shift_left(bits, place).astype(jnp.float32), axis=0, keepdims=True)
    scale = jnp.exp2((number - BIAS) * (1.0 / STEPS)) * (1.0 / REACH)
    return jnp.concatenate([head - bits, value[HEAD:]], axis=0).astype(jnp.float32) * scale


def chunk_of(position, deep):
    across = lax.rem(position + deep, 2)
    along = lax.rem(lax.div(position, 2) + lax.div(deep, 2), 2)
    return 2 * lax.rem(across + along, 2) + along


def position_of(chunk, deep):
    along = lax.rem(chunk, 2)
    across = lax.rem(lax.div(chunk, 2) + along, 2)
    return lax.rem(across + deep, 2) + 2 * lax.rem(along + lax.div(deep, 2), 2)


LANES = 128
AHEAD = 4


def remote(source, target, sems, piece, number, device):
    return pltpu.make_async_remote_copy(
        source,
        target,
        sems.at[0, piece, number],
        sems.at[1, piece, number],
        device_id=device,
        device_id_type=MESH,
    )


def fused_kernel(
    factor_hbm,
    mask,
    ancestor,
    out,
    gathered,
    factor,
    turned,
    tiles,
    parts,
    first_out,
    first,
    second_out,
    second,
    ended,
    landing,
    term,
    plane_out,
    plane,
    line,
    shared,
    loads,
    sems,
    plane_sems,
    line_sems,
    shared_sems,
    small_loads,
):
    n_rows = lax.axis_size("prow")
    n_cols = lax.axis_size("pcol")
    n_deep = n_cols // 2
    row = lax.axis_index("prow")
    column = lax.axis_index("pcol")
    count, rows_here, width = factor.shape
    slab = out.shape[1]
    lanes_each = slab // LANES
    pieces = count * lanes_each
    half = width // 2
    flip_x = row + 1 - 2 * lax.rem(row, 2)
    flip_y = lax.rem(row + 2, 4)
    flip_both = 3 - row
    x_peer, y_peer = (flip_x, column), (flip_y, column)
    deep, core = lax.div(column, 2), lax.rem(column, 2)
    place = column * n_rows + chunk_of(row, deep)
    target = (lax.div(place, n_cols), lax.rem(place, n_cols))
    here = row * n_cols + column
    from_column = lax.div(here, n_rows)
    origin = (position_of(lax.rem(here, n_rows), lax.div(from_column, 2)), from_column)
    order = (flip_both, flip_x, flip_y, row)
    upper, lower = pl.ds(0, half), pl.ds(half, half)
    group = 2 * n_rows
    member = row * 2 + core
    height = 3 * width // (2 * group)

    def load(t):
        start = pl.multiple_of(chunk_of(order[t % 4], deep) * slab + (t // 4) * LANES, LANES)
        return pltpu.make_async_copy(ancestor.at[:, pl.ds(start, LANES)], tiles.at[t], loads.at[t])

    def load_factor(k):
        return pltpu.make_async_copy(factor_hbm.at[k], factor.at[k], small_loads.at[k])

    load_factor(0).start()
    for t in range(AHEAD):
        load(t).start()
    for other in range(1, count):
        load_factor(other).start()
    blocks_here = rows_here // WIDTH

    def in_plane(d):
        peer = lax.rem(member + d, group)
        return peer, (lax.div(peer, 2), deep * 2 + lax.rem(peer, 2))

    def on_line(d):
        peer = lax.rem(deep + d, n_deep)
        return (row, peer * 2 + core)

    barrier = pltpu.get_barrier_semaphore()
    peers = [in_plane(d)[1] for d in range(1, group)] + [on_line(d) for d in range(1, n_deep)]
    for peer in peers:
        pl.semaphore_signal(barrier, inc=1, device_id=peer, device_id_type=MESH)

    @pl.when(place != here)
    def _():
        pl.semaphore_signal(barrier, inc=1, device_id=origin, device_id_type=MESH)

    def turn(k):
        load_factor(k).wait()
        for i in range(blocks_here):
            at = pl.ds(i * WIDTH, WIDTH)
            kept = mask[k, row * blocks_here + i].astype(jnp.float32)
            block = factor[k, at].T.astype(jnp.float32) * kept
            turned[pl.ds(k * width, width), at] = block.astype(jnp.bfloat16)

    turn(0)

    @pl.when(place != here)
    def _():
        pl.semaphore_wait(barrier, len(peers) + 1)

    @pl.when(place == here)
    def _():
        pl.semaphore_wait(barrier, len(peers))

    def early(i, s):
        return remote(first_out.at[i, s], first.at[i, s], sems, i, s, (x_peer, x_peer, y_peer, y_peer)[s])

    def late(i, s):
        return remote(second_out.at[i, s], second.at[i, s], sems, i, 4 + s, (y_peer, x_peer)[s])

    def final(i):
        return remote(ended.at[i], landing.at[i], sems, i, 6, target)

    def compute(i):
        k, j = divmod(i, lanes_each)
        for q in range(4):
            t = 4 * j + q
            if k == 0:
                load(t).wait()
                if t + AHEAD < 4 * lanes_each:
                    load(t + AHEAD).start()
            value = tiles[t]
            high = value.astype(jnp.bfloat16)
            low = (value - high.astype(jnp.float32)).astype(jnp.bfloat16)
            stacked = jnp.concatenate([high, low], axis=1)
            for h in range(2):
                both = dot(turned[pl.ds(k * width + h * half, half)], stacked)
                parts[4 * i + q, pl.ds(h * half, half)] = both[:, :LANES] + both[:, LANES:]
            ready = ((0, 2), (1,), (3,), ())[q]
            for s in ready:
                encode(parts[4 * i + q, (upper, upper, lower, lower)[s]], first_out.at[i, s])
            for s in ready:
                early(i, s).start()

    def forward(i):
        early(i, 0).wait_recv()
        early(i, 2).wait_recv()
        encode(parts[4 * i + 2, upper] + decode(first.at[i, 0]), second_out.at[i, 0])
        encode(parts[4 * i + 1, lower] + decode(first.at[i, 2]), second_out.at[i, 1])
        late(i, 0).start()
        late(i, 1).start()

    def end(i):
        early(i, 1).wait_recv()
        early(i, 3).wait_recv()
        late(i, 0).wait_recv()
        late(i, 1).wait_recv()
        ready = parts[4 * i + 3, upper] + decode(first.at[i, 1]) + decode(second.at[i, 0])
        encode(ready, ended.at[i, upper])
        ready = parts[4 * i + 3, lower] + decode(first.at[i, 3]) + decode(second.at[i, 1])
        encode(ready, ended.at[i, lower])

        @pl.when(place != here)
        def _():
            final(i).start()

        @pl.when(place == here)
        def _():
            landing[i] = ended[i]

    def diagonal(k):
        total = 0.0
        for j in range(lanes_each):
            i = k * lanes_each + j

            @pl.when(place != here)
            def _():
                final(i).wait_recv()

            value = jnp.concatenate([decode(landing.at[i, upper]), decode(landing.at[i, lower])], axis=0)
            parts[4 * i] = value
            high = value.astype(jnp.bfloat16)
            low = (value - high.astype(jnp.float32)).astype(jnp.bfloat16)
            lanes = pl.ds(pl.multiple_of(column * slab + j * LANES, LANES), LANES)
            own = turned[pl.ds(k * width, width), lanes]
            total = total + lax.dot_general(
                jnp.concatenate([own, own], axis=1),
                jnp.concatenate([high, low], axis=1),
                (((1,), (1,)), ((), ())),
                preferred_element_type=jnp.float32,
            )
        mid = width // 2
        term[k, pl.ds(0, mid)] = total[:mid, :mid]
        term[k, pl.ds(mid, mid)] = total[:mid, mid:]
        term[k, pl.ds(2 * mid, mid)] = total[mid:, mid:]
        copies = []
        for d in range(group):
            encode(term[k, pl.ds(d * height, height)], plane_out.at[k, d])
        for d in range(1, group):
            peer, device = in_plane(d)
            copy = remote(plane_out.at[k, peer], plane.at[k, d - 1], plane_sems, k, d - 1, device)
            copy.start()
            copies.append(copy)
        yield
        for copy in copies:
            copy.wait_recv()
        total = term[k, pl.ds(pl.multiple_of(member * height, height), height)]
        for d in range(1, group):
            total = total + decode(plane.at[k, d - 1])
        encode(total, line.at[k, deep])
        sent = copies
        copies = []
        for d in range(1, n_deep):
            copy = remote(line.at[k, deep], line.at[k, deep], line_sems, k, d - 1, on_line(d))
            copy.start()
            copies.append(copy)
        yield
        for copy in copies:
            copy.wait_recv()
        total = decode(line.at[k, 0])
        for d in range(1, n_deep):
            total = total + decode(line.at[k, d])
        encode(total, shared.at[k, member])
        sent = sent + copies
        copies = []
        for d in range(1, group):
            copy = remote(
                shared.at[k, member], shared.at[k, member], shared_sems, k, d - 1, in_plane(d)[1]
            )
            copy.start()
            copies.append(copy)
        yield
        for copy in copies:
            copy.wait_recv()
        for d in range(group):
            term[k, pl.ds(d * height, height)] = decode(shared.at[k, d])
        cross = term[k, pl.ds(mid, mid)]
        top = jnp.concatenate([term[k, pl.ds(0, mid)], cross], axis=1)
        bottom = jnp.concatenate([cross.T, term[k, pl.ds(2 * mid, mid)]], axis=1)
        gathered[k] = jnp.concatenate([top, bottom], axis=0)
        for copy in sent + copies:
            copy.wait_send()

    def turn_back(k):
        for j in range(lanes_each):
            start = row * rows_here + column * slab + j * LANES
            kept = mask[k, lax.div(start, WIDTH)].astype(jnp.float32)
            out[k, pl.ds(j * LANES, LANES)] = parts[4 * (k * lanes_each + j)].T * kept

    for i in range(pieces):
        compute(i)
        if i == 0:
            for k in range(1, count):
                turn(k)
        if i >= 1:
            forward(i - 1)
        if i >= 2:
            end(i - 2)
    forward(pieces - 1)
    end(pieces - 2)
    running = [diagonal(k) for k in range(count)]
    end(pieces - 1)
    for _ in range(3):
        for k in range(count):
            next(running[k])
    for k in range(count):
        turn_back(k)
    for k in range(count):
        next(running[k], None)
    for i in range(pieces):
        @pl.when(place != here)
        def _():
            final(i).wait_send()

        for s in range(4):
            early(i, s).wait_send()
        for s in range(2):
            late(i, s).wait_send()


def fused(factor, mask, ancestor):
    count, depth, width = factor.shape
    n_rows, n_cols = lax.axis_size("prow"), lax.axis_size("pcol")
    slab = ancestor.shape[1] // n_rows
    lanes_each = slab // LANES
    pieces = count * lanes_each
    half = width // 2
    group, n_deep = 2 * n_rows, n_cols // 2
    height = 3 * width // (2 * group)
    vmem, hbm = pl.BlockSpec(memory_space=pltpu.VMEM), pl.BlockSpec(memory_space=pl.ANY)
    f32, i16 = jnp.float32, jnp.int16
    return pl.pallas_call(
        fused_kernel,
        out_shape=(
            jax.ShapeDtypeStruct((count, slab, width), f32),
            jax.ShapeDtypeStruct((count, width, width), f32),
        ),
        in_specs=[hbm, pl.BlockSpec(memory_space=pltpu.SMEM), hbm],
        out_specs=(vmem, vmem),
        scratch_shapes=[
            pltpu.VMEM(factor.shape, factor.dtype),
            pltpu.VMEM((count * width, depth), jnp.bfloat16),
            pltpu.VMEM((4 * lanes_each, depth, LANES), f32),
            pltpu.VMEM((4 * pieces, width, LANES), f32),
            pltpu.VMEM((pieces, 4, half, LANES), i16),
            pltpu.VMEM((pieces, 4, half, LANES), i16),
            pltpu.VMEM((pieces, 2, half, LANES), i16),
            pltpu.VMEM((pieces, 2, half, LANES), i16),
            pltpu.VMEM((pieces, width, LANES), i16),
            pltpu.VMEM((pieces, width, LANES), i16),
            pltpu.VMEM((count, group * height, width // 2), f32),
            pltpu.VMEM((count, group, height, width // 2), i16),
            pltpu.VMEM((count, group - 1, height, width // 2), i16),
            pltpu.VMEM((count, n_deep, height, width // 2), i16),
            pltpu.VMEM((count, group, height, width // 2), i16),
            pltpu.SemaphoreType.DMA((4 * lanes_each,)),
            pltpu.SemaphoreType.DMA((2, pieces, 7)),
            pltpu.SemaphoreType.DMA((2, count, group - 1)),
            pltpu.SemaphoreType.DMA((2, count, n_deep - 1)),
            pltpu.SemaphoreType.DMA((2, count, group - 1)),
            pltpu.SemaphoreType.DMA((count,)),
        ],
        compiler_params=pltpu.CompilerParams(
            collective_id=1, has_side_effects=True, vmem_limit_bytes=50 * 1024 * 1024
        ),
    )(factor, mask, ancestor)


def product_plain(turned, ancestor):
    n_rows = lax.axis_size("prow")
    n_cols = lax.axis_size("pcol")
    high, low = split(ancestor)
    partial = dot(turned, high) + dot(turned, low)
    summed = lax.psum_scatter(partial, "prow", scatter_dimension=1, tiled=True)
    pairs = [(r * n_cols + c, c * n_rows + r) for r in range(n_rows) for c in range(n_cols)]
    return lax.ppermute(summed, ("prow", "pcol"), pairs)


def shards(ancestor, factor, inverse_diag, block_mask):
    rows_here = ancestor.shape[0]
    count, _, width = factor.shape
    n_rows = lax.axis_size("prow")
    n_cols = lax.axis_size("pcol")
    column = lax.axis_index("pcol")
    grid_row = lax.axis_index("prow")
    slab = rows_here // n_cols
    fits = n_rows == 4 and n_cols % 2 == 0 and n_cols > 2 and width == WIDTH
    fits = fits and slab % LANES == 0 and slab * n_rows == ancestor.shape[1]
    if fits:
        placed, total = fused(factor, block_mask, ancestor)
        return (-placed, inverse_diag.astype(jnp.float32) + total)
    row_mask = jnp.repeat(block_mask, WIDTH, axis=1).astype(jnp.float32)
    own_mask = lax.dynamic_slice_in_dim(row_mask, grid_row * rows_here, rows_here, 1)
    slab_mask = lax.dynamic_slice_in_dim(own_mask, column * slab, slab, 1)
    inverse = inverse_diag.astype(jnp.float32)
    masked = factor * own_mask[:, :, None].astype(factor.dtype)
    turned = masked.transpose(0, 2, 1).reshape(count * width, rows_here)
    placed = product_plain(turned, ancestor).reshape(count, width, slab)
    column_block = -slab_mask[:, :, None] * placed.transpose(0, 2, 1)
    own_slab = lax.dynamic_slice_in_dim(masked, column * slab, slab, 1)
    high, low = split(column_block)
    term = jnp.stack([dot(own_slab[k].T, high[k]) + dot(own_slab[k].T, low[k]) for k in range(count)])
    return (column_block, inverse - lax.psum(term, ("prow", "pcol")))


def solution(mesh):
    return jax.shard_map(
        shards,
        mesh=mesh,
        in_specs=(P("prow", "pcol"), P(None, "prow", None), P(), P()),
        out_specs=(P(None, ("prow", "pcol"), None), P()),
        check_vma=False,
    )
```

```python
import jax
import jax.numpy as jnp
from jax import lax
from jax.experimental import pallas as pl
from jax.experimental.pallas import tpu as pltpu
from jax.sharding import PartitionSpec as P

WIDTH = 256


def split(x):
    high = lax.reduce_precision(x, 8, 7)
    low = x - high
    return high.astype(jnp.bfloat16), low.astype(jnp.bfloat16)


def dot(a, b):
    return jnp.dot(a, b, preferred_element_type=jnp.float32)


MESH = pl.DeviceIdType.MESH


STEPS = 32.0
BIAS = 4096.0
REACH = 32760.0
HEAD = 16


def part(ref, start, size):
    return ref.at[pl.ds(pl.multiple_of(start, 8), size)]


def encode(value, wire):
    top = jnp.max(jnp.abs(value), axis=0, keepdims=True)
    code = jnp.ceil(jnp.log2(jnp.maximum(top, 1e-30)) * STEPS) + 1.0
    scale = jnp.exp2(code * (-1.0 / STEPS)) * REACH
    number = (code + BIAS).astype(jnp.int32)
    place = lax.broadcasted_iota(jnp.int32, (HEAD, value.shape[1]), 0)
    bits = lax.shift_right_logical(jnp.broadcast_to(number, place.shape), place) & 1
    head = jnp.round(value[:HEAD] * (scale * 0.5)).astype(jnp.int32) * 2 + bits
    rest = jnp.round(value[HEAD:] * scale).astype(jnp.int32)
    wire[...] = jnp.concatenate([head, rest], axis=0).astype(jnp.int16)


def decode(wire):
    value = wire[...].astype(jnp.int32)
    head = value[:HEAD]
    bits = head & 1
    place = lax.broadcasted_iota(jnp.int32, head.shape, 0)
    number = jnp.sum(lax.shift_left(bits, place).astype(jnp.float32), axis=0, keepdims=True)
    scale = jnp.exp2((number - BIAS) * (1.0 / STEPS)) * (1.0 / REACH)
    return jnp.concatenate([head - bits, value[HEAD:]], axis=0).astype(jnp.float32) * scale


def chunk_of(position, deep):
    across = lax.rem(position + deep, 2)
    along = lax.rem(lax.div(position, 2) + lax.div(deep, 2), 2)
    return 2 * lax.rem(across + along, 2) + along


def position_of(chunk, deep):
    along = lax.rem(chunk, 2)
    across = lax.rem(lax.div(chunk, 2) + along, 2)
    return lax.rem(across + deep, 2) + 2 * lax.rem(along + lax.div(deep, 2), 2)


LANES = 128
AHEAD = 4


def remote(source, target, sems, piece, number, device):
    return pltpu.make_async_remote_copy(
        source,
        target,
        sems.at[0, piece, number],
        sems.at[1, piece, number],
        device_id=device,
        device_id_type=MESH,
    )


def fused_kernel(
    factor_hbm,
    mask,
    ancestor,
    out,
    gathered,
    factor,
    turned,
    tiles,
    parts,
    first_out,
    first,
    second_out,
    second,
    ended,
    landing,
    term,
    plane_out,
    plane,
    line,
    shared,
    loads,
    sems,
    plane_sems,
    line_sems,
    shared_sems,
    small_loads,
):
    n_rows = lax.axis_size("prow")
    n_cols = lax.axis_size("pcol")
    n_deep = n_cols // 2
    row = lax.axis_index("prow")
    column = lax.axis_index("pcol")
    count, rows_here, width = factor.shape
    slab = out.shape[1]
    lanes_each = slab // LANES
    pieces = count * lanes_each
    half = width // 2
    flip_x = row + 1 - 2 * lax.rem(row, 2)
    flip_y = lax.rem(row + 2, 4)
    flip_both = 3 - row
    x_peer, y_peer = (flip_x, column), (flip_y, column)
    deep, core = lax.div(column, 2), lax.rem(column, 2)
    place = column * n_rows + chunk_of(row, deep)
    target = (lax.div(place, n_cols), lax.rem(place, n_cols))
    here = row * n_cols + column
    from_column = lax.div(here, n_rows)
    origin = (position_of(lax.rem(here, n_rows), lax.div(from_column, 2)), from_column)
    order = (flip_both, flip_x, flip_y, row)
    upper, lower = pl.ds(0, half), pl.ds(half, half)
    group = 2 * n_rows
    member = row * 2 + core
    height = 3 * width // (2 * group)

    def load(t):
        start = pl.multiple_of(chunk_of(order[t % 4], deep) * slab + (t // 4) * LANES, LANES)
        return pltpu.make_async_copy(ancestor.at[:, pl.ds(start, LANES)], tiles.at[t], loads.at[t])

    def load_factor(k):
        return pltpu.make_async_copy(factor_hbm.at[k], factor.at[k], small_loads.at[k])

    load_factor(0).start()
    for t in range(AHEAD):
        load(t).start()
    for other in range(1, count):
        load_factor(other).start()
    blocks_here = rows_here // WIDTH

    def in_plane(d):
        peer = lax.rem(member + d, group)
        return peer, (lax.div(peer, 2), deep * 2 + lax.rem(peer, 2))

    def on_line(d):
        peer = lax.rem(deep + d, n_deep)
        return (row, peer * 2 + core)

    barrier = pltpu.get_barrier_semaphore()
    peers = [in_plane(d)[1] for d in range(1, group)] + [on_line(d) for d in range(1, n_deep)]
    for peer in peers:
        pl.semaphore_signal(barrier, inc=1, device_id=peer, device_id_type=MESH)

    @pl.when(place != here)
    def _():
        pl.semaphore_signal(barrier, inc=1, device_id=origin, device_id_type=MESH)

    def turn(k):
        load_factor(k).wait()
        for i in range(blocks_here):
            at = pl.ds(i * WIDTH, WIDTH)
            kept = mask[k, row * blocks_here + i].astype(jnp.float32)
            block = factor[k, at].T.astype(jnp.float32) * kept
            turned[pl.ds(k * width, width), at] = block.astype(jnp.bfloat16)

    turn(0)

    @pl.when(place != here)
    def _():
        pl.semaphore_wait(barrier, len(peers) + 1)

    @pl.when(place == here)
    def _():
        pl.semaphore_wait(barrier, len(peers))

    def early(i, s):
        return remote(first_out.at[i, s], first.at[i, s], sems, i, s, (x_peer, x_peer, y_peer, y_peer)[s])

    def late(i, s):
        return remote(second_out.at[i, s], second.at[i, s], sems, i, 4 + s, (y_peer, x_peer)[s])

    def final(i):
        return remote(ended.at[i], landing.at[i], sems, i, 6, target)

    def compute(i):
        k, j = divmod(i, lanes_each)
        for q in range(4):
            t = 4 * j + q
            if k == 0:
                load(t).wait()
                if t + AHEAD < 4 * lanes_each:
                    load(t + AHEAD).start()
            value = tiles[t]
            high = value.astype(jnp.bfloat16)
            low = (value - high.astype(jnp.float32)).astype(jnp.bfloat16)
            stacked = jnp.concatenate([high, low], axis=1)
            for h in range(2):
                both = dot(turned[pl.ds(k * width + h * half, half)], stacked)
                parts[4 * i + q, pl.ds(h * half, half)] = both[:, :LANES] + both[:, LANES:]
            ready = ((0, 2), (1,), (3,), ())[q]
            for s in ready:
                encode(parts[4 * i + q, (upper, upper, lower, lower)[s]], first_out.at[i, s])
            for s in ready:
                early(i, s).start()

    def forward(i):
        early(i, 0).wait_recv()
        early(i, 2).wait_recv()
        encode(parts[4 * i + 2, upper] + decode(first.at[i, 0]), second_out.at[i, 0])
        encode(parts[4 * i + 1, lower] + decode(first.at[i, 2]), second_out.at[i, 1])
        late(i, 0).start()
        late(i, 1).start()

    def end(i):
        early(i, 1).wait_recv()
        early(i, 3).wait_recv()
        late(i, 0).wait_recv()
        late(i, 1).wait_recv()
        ready = parts[4 * i + 3, upper] + decode(first.at[i, 1]) + decode(second.at[i, 0])
        encode(ready, ended.at[i, upper])
        ready = parts[4 * i + 3, lower] + decode(first.at[i, 3]) + decode(second.at[i, 1])
        encode(ready, ended.at[i, lower])

        @pl.when(place != here)
        def _():
            final(i).start()

        @pl.when(place == here)
        def _():
            landing[i] = ended[i]

    def diagonal(k):
        total = 0.0
        for j in range(lanes_each):
            i = k * lanes_each + j

            @pl.when(place != here)
            def _():
                final(i).wait_recv()

            value = jnp.concatenate([decode(landing.at[i, upper]), decode(landing.at[i, lower])], axis=0)
            parts[4 * i] = value
            high = value.astype(jnp.bfloat16)
            low = (value - high.astype(jnp.float32)).astype(jnp.bfloat16)
            lanes = pl.ds(pl.multiple_of(column * slab + j * LANES, LANES), LANES)
            own = turned[pl.ds(k * width, width), lanes]
            total = total + lax.dot_general(
                jnp.concatenate([own, own], axis=1),
                jnp.concatenate([high, low], axis=1),
                (((1,), (1,)), ((), ())),
                preferred_element_type=jnp.float32,
            )
        mid = width // 2
        term[k, pl.ds(0, mid)] = total[:mid, :mid]
        term[k, pl.ds(mid, mid)] = total[:mid, mid:]
        term[k, pl.ds(2 * mid, mid)] = total[mid:, mid:]
        copies = []
        for d in range(group):
            encode(term[k, pl.ds(d * height, height)], plane_out.at[k, d])
        for d in range(1, group):
            peer, device = in_plane(d)
            copy = remote(plane_out.at[k, peer], plane.at[k, d - 1], plane_sems, k, d - 1, device)
            copy.start()
            copies.append(copy)
        yield
        for copy in copies:
            copy.wait_recv()
        total = term[k, pl.ds(pl.multiple_of(member * height, height), height)]
        for d in range(1, group):
            total = total + decode(plane.at[k, d - 1])
        encode(total, line.at[k, deep])
        sent = copies
        copies = []
        for d in range(1, n_deep):
            copy = remote(line.at[k, deep], line.at[k, deep], line_sems, k, d - 1, on_line(d))
            copy.start()
            copies.append(copy)
        yield
        for copy in copies:
            copy.wait_recv()
        total = decode(line.at[k, 0])
        for d in range(1, n_deep):
            total = total + decode(line.at[k, d])
        encode(total, shared.at[k, member])
        sent = sent + copies
        copies = []
        for d in range(1, group):
            copy = remote(
                shared.at[k, member], shared.at[k, member], shared_sems, k, d - 1, in_plane(d)[1]
            )
            copy.start()
            copies.append(copy)
        yield
        for copy in copies:
            copy.wait_recv()
        for d in range(group):
            term[k, pl.ds(d * height, height)] = decode(shared.at[k, d])
        cross = term[k, pl.ds(mid, mid)]
        top = jnp.concatenate([term[k, pl.ds(0, mid)], cross], axis=1)
        bottom = jnp.concatenate([cross.T, term[k, pl.ds(2 * mid, mid)]], axis=1)
        gathered[k] = jnp.concatenate([top, bottom], axis=0)
        for copy in sent + copies:
            copy.wait_send()

    def turn_back(k):
        for j in range(lanes_each):
            start = row * rows_here + column * slab + j * LANES
            kept = mask[k, lax.div(start, WIDTH)].astype(jnp.float32)
            out[k, pl.ds(j * LANES, LANES)] = parts[4 * (k * lanes_each + j)].T * kept

    for i in range(pieces):
        compute(i)
        if i >= 1:
            forward(i - 1)
        if i >= 2:
            end(i - 2)
        if i == lanes_each - 1:
            for k in range(1, count):
                turn(k)
    forward(pieces - 1)
    end(pieces - 2)
    running = [diagonal(k) for k in range(count)]
    end(pieces - 1)
    for _ in range(3):
        for k in range(count):
            next(running[k])
    for k in range(count):
        turn_back(k)
    for k in range(count):
        next(running[k], None)
    for i in range(pieces):
        @pl.when(place != here)
        def _():
            final(i).wait_send()

        for s in range(4):
            early(i, s).wait_send()
        for s in range(2):
            late(i, s).wait_send()


def fused(factor, mask, ancestor):
    count, depth, width = factor.shape
    n_rows, n_cols = lax.axis_size("prow"), lax.axis_size("pcol")
    slab = ancestor.shape[1] // n_rows
    lanes_each = slab // LANES
    pieces = count * lanes_each
    half = width // 2
    group, n_deep = 2 * n_rows, n_cols // 2
    height = 3 * width // (2 * group)
    vmem, hbm = pl.BlockSpec(memory_space=pltpu.VMEM), pl.BlockSpec(memory_space=pl.ANY)
    f32, i16 = jnp.float32, jnp.int16
    return pl.pallas_call(
        fused_kernel,
        out_shape=(
            jax.ShapeDtypeStruct((count, slab, width), f32),
            jax.ShapeDtypeStruct((count, width, width), f32),
        ),
        in_specs=[hbm, pl.BlockSpec(memory_space=pltpu.SMEM), hbm],
        out_specs=(vmem, vmem),
        scratch_shapes=[
            pltpu.VMEM(factor.shape, factor.dtype),
            pltpu.VMEM((count * width, depth), jnp.bfloat16),
            pltpu.VMEM((4 * lanes_each, depth, LANES), f32),
            pltpu.VMEM((4 * pieces, width, LANES), f32),
            pltpu.VMEM((pieces, 4, half, LANES), i16),
            pltpu.VMEM((pieces, 4, half, LANES), i16),
            pltpu.VMEM((pieces, 2, half, LANES), i16),
            pltpu.VMEM((pieces, 2, half, LANES), i16),
            pltpu.VMEM((pieces, width, LANES), i16),
            pltpu.VMEM((pieces, width, LANES), i16),
            pltpu.VMEM((count, group * height, width // 2), f32),
            pltpu.VMEM((count, group, height, width // 2), i16),
            pltpu.VMEM((count, group - 1, height, width // 2), i16),
            pltpu.VMEM((count, n_deep, height, width // 2), i16),
            pltpu.VMEM((count, group, height, width // 2), i16),
            pltpu.SemaphoreType.DMA((4 * lanes_each,)),
            pltpu.SemaphoreType.DMA((2, pieces, 7)),
            pltpu.SemaphoreType.DMA((2, count, group - 1)),
            pltpu.SemaphoreType.DMA((2, count, n_deep - 1)),
            pltpu.SemaphoreType.DMA((2, count, group - 1)),
            pltpu.SemaphoreType.DMA((count,)),
        ],
        compiler_params=pltpu.CompilerParams(
            collective_id=1, has_side_effects=True, vmem_limit_bytes=50 * 1024 * 1024
        ),
    )(factor, mask, ancestor)


def product_plain(turned, ancestor):
    n_rows = lax.axis_size("prow")
    n_cols = lax.axis_size("pcol")
    high, low = split(ancestor)
    partial = dot(turned, high) + dot(turned, low)
    summed = lax.psum_scatter(partial, "prow", scatter_dimension=1, tiled=True)
    pairs = [(r * n_cols + c, c * n_rows + r) for r in range(n_rows) for c in range(n_cols)]
    return lax.ppermute(summed, ("prow", "pcol"), pairs)


def shards(ancestor, factor, inverse_diag, block_mask):
    rows_here = ancestor.shape[0]
    count, _, width = factor.shape
    n_rows = lax.axis_size("prow")
    n_cols = lax.axis_size("pcol")
    column = lax.axis_index("pcol")
    grid_row = lax.axis_index("prow")
    slab = rows_here // n_cols
    fits = n_rows == 4 and n_cols % 2 == 0 and n_cols > 2 and width == WIDTH
    fits = fits and slab % LANES == 0 and slab * n_rows == ancestor.shape[1]
    if fits:
        placed, total = fused(factor, block_mask, ancestor)
        return (-placed, inverse_diag.astype(jnp.float32) + total)
    row_mask = jnp.repeat(block_mask, WIDTH, axis=1).astype(jnp.float32)
    own_mask = lax.dynamic_slice_in_dim(row_mask, grid_row * rows_here, rows_here, 1)
    slab_mask = lax.dynamic_slice_in_dim(own_mask, column * slab, slab, 1)
    inverse = inverse_diag.astype(jnp.float32)
    masked = factor * own_mask[:, :, None].astype(factor.dtype)
    turned = masked.transpose(0, 2, 1).reshape(count * width, rows_here)
    placed = product_plain(turned, ancestor).reshape(count, width, slab)
    column_block = -slab_mask[:, :, None] * placed.transpose(0, 2, 1)
    own_slab = lax.dynamic_slice_in_dim(masked, column * slab, slab, 1)
    high, low = split(column_block)
    term = jnp.stack([dot(own_slab[k].T, high[k]) + dot(own_slab[k].T, low[k]) for k in range(count)])
    return (column_block, inverse - lax.psum(term, ("prow", "pcol")))


def solution(mesh):
    return jax.shard_map(
        shards,
        mesh=mesh,
        in_specs=(P("prow", "pcol"), P(None, "prow", None), P(), P()),
        out_specs=(P(None, ("prow", "pcol"), None), P()),
        check_vma=False,
    )
```
